32 devices in a mesh: section: 4 (over z), space: 8 (over y, x, core).
Axes of the slice: x: 2, y: 2, z: 4, core: 2. Of those that a mesh axis runs over, the one named last changes fastest.
Arguments:
- act_in: bfloat16 [4, 4096, 512], P('section', 'space'), may hold values from -6 to 6
- stash: bfloat16 [4, 4, 4096, 512], P('section', None, 'space'), may hold values from -6 to 6
- plan: int32 [4], P('section'), may hold values from 0 to 3
- grad_in: bfloat16 [4, 4096, 512], P('section', 'space'), may hold values from -6 to 6
- fwd_owner: int32 [4, 4096], P('section', 'space'), may hold values from 0 to 7, as said below
- stash_owner: int32 [4, 4, 4096], P('section', None, 'space'), may hold values from 0 to 7, as said below
- ln_gain: float32 [4, 512], P('section'), may hold values from 0.5 to 1.5
- qkv_weight: bfloat16 [4, 512, 1536], P('section')
- proj_weight: bfloat16 [4, 512, 512], P('section'), may hold values from -1 to 1
Outputs:
- act_out: bfloat16 [4, 4096, 512], P('section', 'space')
- grad_out: bfloat16 [4, 4096, 512], P('section', 'space')
The draws below stay inside these ranges and needn't reach their ends.
Inputs may be any that keep to these rules, and one draw needn't show every extreme that they name: `fwd_owner`: within each group of 512 rows of one list, owners never decrease; each group sends 128 rows to a quarter of the owners, 64 rows to half of them and none to the rest; in each list one owner gets 128 rows from every group. `stash_owner`: same law for each section and stored microbatch, independently drawn.
All inputs are finite; a program needn't handle non-finite values.
Results may differ from the reference program's by a relative error of at most 0.004.
The reference program's roundings to bfloat16 on the way count: a program that leaves them out, or rounds other values in their place, can miss the bound.
Values may be sent and summed in bfloat16 or wider, within the bound.
A program may use at most 128 MiB of HBM per device.

```python
import math
import jax
import jax.numpy as jnp
from jax import lax

D = 512
HEADS = 32
PATCH = 1024
STASH = 4
PTS_DEV = 512
CAP = 128
POINTS = 4096
N_SECTION = 4
N_SPACE = 8


def cloud(key):
    groups = N_SPACE
    rows = PTS_DEV
    cap = PATCH // N_SPACE
    labels = jnp.arange(groups, dtype=jnp.int32)
    share = jnp.where(labels < groups // 4, cap, jnp.where(labels < 3 * groups // 4, cap // 2, 0)).astype(jnp.int32)
    target = jax.random.randint(jax.random.fold_in(key, 7), (), 0, groups).astype(jnp.int32)

    def one_group(subkey):
        order = jax.random.permutation(subkey, groups).astype(jnp.int32)
        where_target = jnp.argmax(order == target)
        leading = order[0]
        order = order.at[where_target].set(leading).at[0].set(target)
        counts = jnp.zeros((groups,), jnp.int32).at[order].set(share)
        return jnp.repeat(labels, counts, total_repeat_length=rows)
    subkeys = jax.random.split(jax.random.fold_in(key, 11), groups)
    return jax.vmap(one_group)(subkeys).reshape(-1).astype(jnp.int32)


def draw_fwd_owner(key, part):
    subkeys = jax.random.split(jax.random.fold_in(key, 1), N_SECTION)
    return jax.vmap(cloud)(subkeys)


def draw_stash_owner(key, part):
    subkeys = jax.random.split(jax.random.fold_in(key, 2), N_SECTION * STASH)
    return jax.vmap(cloud)(subkeys).reshape(N_SECTION, STASH, POINTS)


def draw_qkv_weight(key, part):
    base_key = jax.random.fold_in(key, 3)
    column = jnp.arange(3 * D, dtype=jnp.int32)
    query_key = column < 2 * D
    values = jnp.clip(jax.random.normal(base_key, (N_SECTION, D, 3 * D), jnp.float32), -4.0, 4.0)
    factor = jnp.where(query_key, 1.25, 1.0)
    return (values * factor[None, None, :] / jnp.sqrt(jnp.float32(D))).astype(jnp.bfloat16)


def touch_ends(array, key, smallest, high):
    dims = array.shape
    place = [jax.random.randint(jax.random.fold_in(key, axis), (), 0, dims[axis]) for axis in range(len(dims))]
    array = array.at[tuple(place)].set(smallest)
    longest = dims.index(max(dims))
    place[longest] = (place[longest] + 1) % dims[longest]
    return array.at[tuple(place)].set(high)


def levels(stream_key, extent, cuts, smallest, high):
    factor_of, own = 1.0, jax.random.fold_in(stream_key, 6)
    for axis_at, blocks in cuts:
        steps = jnp.exp(jax.random.uniform(jax.random.fold_in(own, axis_at), (blocks,), jnp.float32, smallest / len(cuts), high / len(cuts)))
        factor_of = factor_of * jnp.repeat(steps, extent[axis_at] // blocks).reshape([-1 if axis == axis_at else 1 for axis in range(len(extent))])
    return factor_of


def normal_values(key, dims, scale, most, shards=(), held_as=jnp.bfloat16):
    values = scale * jax.random.normal(key, dims, jnp.float32)
    if shards:
        values = values * levels(key, dims, shards, -0.22, 0.18)
    return jnp.clip(values, -most, most).astype(held_as)


def setup_inputs(seed: int = 0) -> dict:
    key_of = jax.random.split(jax.random.key(seed), 10)
    act_in = normal_values(key_of[0], (N_SECTION, POINTS, D), 1.0, 6.0, ((0, 4), (1, 8)))
    stash = normal_values(key_of[1], (N_SECTION, STASH, POINTS, D), 1.0, 6.0, ((0, 4), (2, 8)))
    plan = touch_ends(jax.random.randint(key_of[2], (N_SECTION,), 0, STASH), jax.random.fold_in(key_of[2], 1), 0, STASH - 1).astype(jnp.int32)
    grad_in = normal_values(key_of[3], (N_SECTION, POINTS, D), 1.0, 6.0, ((0, 4), (1, 8)))
    fwd_owner = draw_fwd_owner(jax.random.fold_in(key_of[9], 71), 0)
    stash_owner = draw_stash_owner(jax.random.fold_in(key_of[9], 71), 0)
    ln_gain = jnp.clip(1.0 + 0.1 * jax.random.normal(key_of[6], (N_SECTION, D), jnp.float32), 0.5, 1.5)
    qkv_weight = draw_qkv_weight(jax.random.fold_in(key_of[9], 71), 0)
    proj_weight = normal_values(key_of[8], (N_SECTION, D, D), (D // 16) ** -0.5, 1.0, ((0, 4),))
    return {"act_in": act_in, "stash": stash, "plan": plan, "grad_in": grad_in, "fwd_owner": fwd_owner, "stash_owner": stash_owner, "ln_gain": ln_gain, "qkv_weight": qkv_weight, "proj_weight": proj_weight}


EPS = 1e-05
NEG = -1e+30

def normalize(rows_in, gain):
    values = rows_in.astype(jnp.float32)
    center = values - lax.optimization_barrier(jnp.mean(values, axis=-1, keepdims=True))
    spread = lax.optimization_barrier(jnp.mean(center * center, axis=-1, keepdims=True))
    return center * lax.rsqrt(spread + EPS) * gain

def head_probs(query, key_rows, live, scale):
    score = jnp.dot(query, key_rows.T, preferred_element_type=jnp.float32) * scale
    score = jnp.where(live[None, :], score, NEG)
    top = lax.optimization_barrier(jnp.max(score, axis=1, keepdims=True))
    expd = jnp.exp(score - top)
    return expd / lax.optimization_barrier(jnp.sum(expd, axis=1, keepdims=True))

def attend(patch, live, heads):
    width = patch.shape[1] // 3
    head_dim = width // heads
    scale = 1.0 / math.sqrt(head_dim)

    def one_head(head_index, totals):
        start = head_index * head_dim
        query = lax.dynamic_slice_in_dim(patch, start, head_dim, 1)
        key_rows = lax.dynamic_slice_in_dim(patch, width + start, head_dim, 1)
        value_rows = lax.dynamic_slice_in_dim(patch, 2 * width + start, head_dim, 1)
        probs = head_probs(query, key_rows, live, scale).astype(jnp.bfloat16)
        result = jnp.dot(probs, value_rows, preferred_element_type=jnp.float32)
        return lax.dynamic_update_slice_in_dim(totals, result, start, 1)
    return lax.fori_loop(0, heads, one_head, jnp.zeros((patch.shape[0], width), jnp.float32))

def attend_grad(patch, live, upstream, heads):
    width = patch.shape[1] // 3
    head_dim = width // heads
    scale = 1.0 / math.sqrt(head_dim)

    def one_head(head_index, totals):
        start = head_index * head_dim
        query = lax.dynamic_slice_in_dim(patch, start, head_dim, 1)
        key_rows = lax.dynamic_slice_in_dim(patch, width + start, head_dim, 1)
        value_rows = lax.dynamic_slice_in_dim(patch, 2 * width + start, head_dim, 1)
        out_grad = lax.dynamic_slice_in_dim(upstream, start, head_dim, 1)
        probs = head_probs(query, key_rows, live, scale)
        rounded = probs.astype(jnp.bfloat16)
        prob_grad = jnp.dot(out_grad, value_rows.T, preferred_element_type=jnp.float32)
        value_grad = jnp.dot(rounded.T, out_grad, preferred_element_type=jnp.float32)
        delta = lax.optimization_barrier(jnp.sum(prob_grad * probs, axis=1, keepdims=True))
        score_grad = (probs * (prob_grad - delta) * scale).astype(jnp.bfloat16)
        query_grad = jnp.dot(score_grad, key_rows, preferred_element_type=jnp.float32)
        key_grad = jnp.dot(score_grad.T, query, preferred_element_type=jnp.float32)
        totals = lax.dynamic_update_slice_in_dim(totals, query_grad, start, 1)
        totals = lax.dynamic_update_slice_in_dim(totals, key_grad, width + start, 1)
        return lax.dynamic_update_slice_in_dim(totals, value_grad, 2 * width + start, 1)
    return lax.fori_loop(0, heads, one_head, jnp.zeros((patch.shape[0], 3 * width), jnp.float32))

def layout(owners, groups, cap):
    rows = owners.shape[0] // groups
    grid = owners.reshape(groups, rows).astype(jnp.int32)
    labels = jnp.arange(groups, dtype=jnp.int32)
    onehot = (grid[:, :, None] == labels[None, None, :]).astype(jnp.int32)
    counts = lax.optimization_barrier(jnp.sum(onehot, axis=1)).astype(jnp.int32)
    offsets = (jnp.cumsum(counts, axis=1) - counts).astype(jnp.int32)
    slots = jnp.arange(cap, dtype=jnp.int32)
    first = (labels[:, None] * rows + offsets).astype(jnp.int32)
    valid = slots[None, None, :] < counts.T[:, :, None]
    index = jnp.where(valid, first.T[:, :, None] + slots[None, None, :], 0).astype(jnp.int32)
    rank = (jnp.arange(rows, dtype=jnp.int32)[None, :] - lax.optimization_barrier(jnp.sum(onehot * offsets[:, None, :], axis=2))).astype(jnp.int32)
    back = (grid * (groups * cap) + labels[:, None] * cap + rank).astype(jnp.int32)
    return (index.reshape(groups, groups * cap), valid.reshape(groups, groups * cap), back.reshape(-1))

def pack_rows(source, index, valid):
    picked = jnp.take(source, index.reshape(-1), axis=0).reshape(index.shape + (source.shape[1],))
    return jnp.where(valid[..., None], picked, jnp.zeros((), source.dtype))

def reference(act_in, stash, plan, grad_in, fwd_owner, stash_owner, ln_gain, qkv_weight, proj_weight):
    outputs = []
    gradients = []
    for section_index in range(N_SECTION):
        rows_in = act_in[section_index]
        gain = ln_gain[section_index]
        w_qkv = qkv_weight[section_index]
        w_proj = proj_weight[section_index]
        normed = normalize(rows_in, gain).astype(jnp.bfloat16)
        projected = jnp.dot(normed, w_qkv, preferred_element_type=jnp.float32).astype(jnp.bfloat16)
        index, valid, back = layout(fwd_owner[section_index], N_SPACE, CAP)
        patches = pack_rows(projected, index, valid)
        attended = lax.map(lambda packed: attend(packed[0], packed[1], HEADS).astype(jnp.bfloat16), (patches, valid))
        att_rows = jnp.take(attended.reshape(-1, D), back, axis=0)
        mixed = rows_in.astype(jnp.float32) + jnp.dot(att_rows, w_proj, preferred_element_type=jnp.float32)
        outputs.append(mixed.astype(jnp.bfloat16))
        pick = plan[section_index]
        stored = lax.dynamic_index_in_dim(stash[section_index], pick, 0, keepdims=False)
        stored_owners = lax.dynamic_index_in_dim(stash_owner[section_index], pick, 0, keepdims=False)
        upstream = grad_in[section_index]
        normed_b = normalize(stored, gain).astype(jnp.bfloat16)
        projected_b = jnp.dot(normed_b, w_qkv, preferred_element_type=jnp.float32).astype(jnp.bfloat16)
        out_grad = jnp.dot(upstream, w_proj.T, preferred_element_type=jnp.float32).astype(jnp.bfloat16)
        index_b, valid_b, back_b = layout(stored_owners, N_SPACE, CAP)
        patches_b = pack_rows(projected_b, index_b, valid_b)
        grads_b = pack_rows(out_grad, index_b, valid_b)
        qkv_grads = lax.map(lambda packed: attend_grad(packed[0], packed[1], packed[2], HEADS).astype(jnp.bfloat16), (patches_b, valid_b, grads_b))
        grad_rows = jnp.take(qkv_grads.reshape(-1, 3 * D), back_b, axis=0)
        normed_grad = jnp.dot(grad_rows, w_qkv.T, preferred_element_type=jnp.float32)
        unused, pull = jax.vjp(lambda values: normalize(values, gain), stored.astype(jnp.float32))
        input_grad = upstream.astype(jnp.float32) + pull(normed_grad)[0]
        gradients.append(input_grad.astype(jnp.bfloat16))
    blank = jnp.zeros((POINTS, D), jnp.bfloat16)
    act_out = jnp.stack([blank] + outputs[:-1])
    grad_out = jnp.stack(gradients[1:] + [blank])
    return (act_out, grad_out)
```

```python
import functools
import math

import jax
import jax.numpy as jnp
from jax import lax
from jax.experimental import pallas as pl
from jax.experimental.pallas import tpu as pltpu
from jax.sharding import PartitionSpec as P

HEADS = 32
EPS = 1e-05
NEG = -1e30
QT = 128
KT = 256
PATCH = 1024
VMEM_LIMIT = 56 * 1024 * 1024
F32 = jnp.float32
BF16 = jnp.bfloat16
NT = (((1,), (1,)), ((), ()))
NN = (((1,), (0,)), ((), ()))


def dot(a, b, dims=NN):
    return lax.dot_general(a, b, dims, preferred_element_type=F32)


def passed_along(value, axis, by):
    size = lax.axis_size(axis)
    pairs = [(i, i + by) for i in range(size) if 0 <= i + by < size]
    return lax.ppermute(value, axis, pairs)


def centered(values):
    center = values - jnp.mean(values, axis=-1, keepdims=True)
    spread = jnp.mean(center * center, axis=-1, keepdims=True)
    return center, lax.rsqrt(spread + EPS)


def project_kernel(groups, hw, rows_ref, gain_ref, wqkv_ref, out_ref, y_ref):
    width = rows_ref.shape[1]
    center, inv = centered(rows_ref[...].astype(F32))
    normed = (center * inv * gain_ref[...]).astype(BF16)
    y_ref[...] = dot(normed, wqkv_ref[...]).astype(BF16)
    for g in range(groups):
        out_ref[g, :, 0:hw] = y_ref[:, width + g * hw:width + (g + 1) * hw]
        out_ref[g, :, hw:2 * hw] = y_ref[:, 2 * width + g * hw:2 * width + (g + 1) * hw]
        out_ref[g, :, 2 * hw:3 * hw] = y_ref[:, g * hw:(g + 1) * hw]


def project_grad_kernel(
    groups, hw, pick_ref, rows_ref, up_ref, gain_ref, wqkv_ref, wproj_ref, out_ref, y_ref, d_ref
):
    width = up_ref.shape[1]
    center, inv = centered(rows_ref[0].astype(F32))
    normed = (center * inv * gain_ref[...]).astype(BF16)
    y_ref[...] = dot(normed, wqkv_ref[...]).astype(BF16)
    d_ref[...] = dot(up_ref[...], wproj_ref[...], NT).astype(BF16)
    for g in range(groups):
        out_ref[g, :, 0:hw] = y_ref[:, width + g * hw:width + (g + 1) * hw]
        out_ref[g, :, hw:2 * hw] = y_ref[:, 2 * width + g * hw:2 * width + (g + 1) * hw]
        out_ref[g, :, 2 * hw:3 * hw] = y_ref[:, g * hw:(g + 1) * hw]
        out_ref[g, :, 3 * hw:4 * hw] = d_ref[:, g * hw:(g + 1) * hw]


def stacked(tile, head_dim, heads, offset):
    lane = lax.broadcasted_iota(jnp.int32, tile.shape, 1)
    zero = jnp.zeros_like(tile)
    parts = []
    for h in range(heads):
        low = offset + h * head_dim
        parts.append(jnp.where((lane >= low) & (lane < low + head_dim), tile, zero))
    return jnp.concatenate(parts, axis=0)


def own_blocks(wide, head_dim, heads):
    picked = [
        wide[h * head_dim:(h + 1) * head_dim, h * QT:(h + 1) * QT] for h in range(heads)
    ]
    return jnp.concatenate(picked, axis=0).T


def each_block(n_blocks, per_group, blk, body):
    def step(b, carry):
        body(b, b // per_group, pl.multiple_of((b % per_group) * blk, blk))
        return carry

    lax.fori_loop(0, n_blocks, step, 0)


def each_patch(groups, blk, start_ref, body):
    def step(o, carry):
        first = start_ref[o]
        live = (start_ref[o + 1] - first) * blk
        base = pl.multiple_of(first * blk, blk)
        for slots in range(KT, PATCH + 1, KT):
            @pl.when((live > slots - KT) & (live <= slots))
            def _():
                body(slots, base, live)

        return carry

    lax.fori_loop(0, groups, step, 0)


def probs_of(scores, live):
    tiles = list(scores)
    low = (len(tiles) - 1) * KT
    row = lax.broadcasted_iota(jnp.int32, tiles[-1].shape, 0) + low
    tiles[-1] = jnp.where(row < live, tiles[-1], NEG)
    top = functools.reduce(jnp.maximum, [jnp.max(t, axis=0, keepdims=True) for t in tiles])
    expd = [jnp.exp(t - top) for t in tiles]
    total = functools.reduce(jnp.add, [jnp.sum(t, axis=0, keepdims=True) for t in expd])
    inv = 1.0 / total
    return [t * inv for t in expd]


def attend_kernel(
    groups, blk, hw, head_dim, pos_ref, start_ref, x_ref, out_ref, kv, qs, res, kvt, pb
):
    heads = hw // head_dim
    scale = 1.0 / math.sqrt(head_dim)
    rows = x_ref.shape[1]
    per_group = rows // blk
    total = groups * rows

    kv[pl.ds(total, KT), :] = jnp.zeros((KT, 2 * hw), BF16)
    qs[pl.ds(total, KT), :] = jnp.zeros((KT, hw), BF16)

    def place(b, g, r):
        to = pl.multiple_of(pos_ref[b] * blk, blk)
        kv[pl.ds(to, blk), :] = x_ref[g, pl.ds(r, blk), 0:2 * hw]
        qs[pl.ds(to, blk), :] = x_ref[g, pl.ds(r, blk), 2 * hw:3 * hw]

    each_block(groups * per_group, per_group, blk, place)

    def patch(slots, base, live):
        kvt[:, 0:slots] = kv[pl.ds(base, slots), :].T

        def chunk(c, carry):
            at = pl.multiple_of(base + c * QT, blk)
            q = (qs[pl.ds(at, QT), :].astype(F32) * scale).astype(BF16)
            q_st = stacked(q, head_dim, heads, 0)
            if hw < kv.shape[1]:
                q_st = jnp.concatenate([q_st, jnp.zeros_like(q_st)], axis=1)
            scores = [
                dot(kv[pl.ds(pl.multiple_of(base + t, blk), KT), :], q_st, NT)
                for t in range(0, slots, KT)
            ]
            for t, p in enumerate(probs_of(scores, live)):
                pb[t * KT:(t + 1) * KT, :] = p.astype(BF16)
            wide = dot(kvt[hw:2 * hw, 0:slots], pb[0:slots, :])
            res[pl.ds(at, QT), :] = own_blocks(wide, head_dim, heads).astype(BF16)
            return carry

        lax.fori_loop(0, (live + QT - 1) // QT, chunk, 0)

    each_patch(groups, blk, start_ref, patch)

    def back(b, g, r):
        at = pl.multiple_of(pos_ref[b] * blk, blk)
        out_ref[g, pl.ds(r, blk), :] = res[pl.ds(at, blk), :]

    each_block(groups * per_group, per_group, blk, back)


def attend_grad_kernel(
    groups, blk, hw, head_dim, pos_ref, start_ref, x_ref, out_ref, kv, qd, dq, dkv, kvt, both, acc
):
    heads = hw // head_dim
    scale = 1.0 / math.sqrt(head_dim)
    rows = x_ref.shape[1]
    per_group = rows // blk
    total = groups * rows
    span = heads * QT

    kv[pl.ds(total, KT), :] = jnp.zeros((KT, 2 * hw), BF16)
    qd[pl.ds(total, KT), :] = jnp.zeros((KT, 2 * hw), BF16)

    def place(b, g, r):
        to = pl.multiple_of(pos_ref[b] * blk, blk)
        kv[pl.ds(to, blk), :] = x_ref[g, pl.ds(r, blk), 0:2 * hw]
        qd[pl.ds(to, blk), :] = x_ref[g, pl.ds(r, blk), 2 * hw:4 * hw]

    each_block(groups * per_group, per_group, blk, place)

    def patch(slots, base, live):
        kvt[:, 0:slots] = kv[pl.ds(base, slots), :].T
        acc[0:slots, :] = jnp.zeros((slots, 2 * hw), F32)

        def chunk(c, carry):
            at = pl.multiple_of(base + c * QT, blk)
            tile = qd[pl.ds(at, QT), :]
            q_st = stacked((tile.astype(F32) * scale).astype(BF16), head_dim, heads, 0)
            row = lax.broadcasted_iota(jnp.int32, tile.shape, 0) + c * QT
            d_st = stacked(jnp.where(row < live, tile, jnp.zeros_like(tile)), head_dim, heads, hw)
            keys = [
                kv[pl.ds(pl.multiple_of(base + t, blk), KT), :] for t in range(0, slots, KT)
            ]
            probs = probs_of([dot(k, q_st, NT) for k in keys], live)
            grads = [dot(k, d_st, NT) for k in keys]
            delta = functools.reduce(
                jnp.add, [jnp.sum(p * g, axis=0, keepdims=True) for p, g in zip(probs, grads)]
            )
            for t, (p, g) in enumerate(zip(probs, grads)):
                both[t * KT:(t + 1) * KT, 0:span] = (p * (g - delta)).astype(BF16)
                both[t * KT:(t + 1) * KT, span:2 * span] = p.astype(BF16)
            right = jnp.concatenate([q_st, d_st], axis=0)
            acc[0:slots, :] += dot(both[0:slots, :], right)
            wide = dot(kvt[0:hw, 0:slots], both[0:slots, 0:span]) * scale
            dq[pl.ds(at, QT), :] = own_blocks(wide, head_dim, heads).astype(BF16)
            return carry

        lax.fori_loop(0, (live + QT - 1) // QT, chunk, 0)
        dkv[pl.ds(base, slots), :] = acc[0:slots, :].astype(BF16)

    each_patch(groups, blk, start_ref, patch)

    def back(b, g, r):
        at = pl.multiple_of(pos_ref[b] * blk, blk)
        out_ref[g, pl.ds(r, blk), 0:2 * hw] = dkv[pl.ds(at, blk), :]
        out_ref[g, pl.ds(r, blk), 2 * hw:3 * hw] = dq[pl.ds(at, blk), :]

    each_block(groups * per_group, per_group, blk, back)


def mix_kernel(groups, hw, att_ref, rows_ref, wproj_ref, out_ref, a_ref):
    for g in range(groups):
        a_ref[:, g * hw:(g + 1) * hw] = att_ref[g]
    mixed = rows_ref[...].astype(F32) + dot(a_ref[...], wproj_ref[...])
    out_ref[...] = mixed.astype(BF16)


def input_grad_kernel(
    groups, hw, pick_ref, dqkv_ref, rows_ref, up_ref, gain_ref, wqkv_ref, out_ref, y_ref
):
    width = up_ref.shape[1]
    for g in range(groups):
        y_ref[:, width + g * hw:width + (g + 1) * hw] = dqkv_ref[g, :, 0:hw]
        y_ref[:, 2 * width + g * hw:2 * width + (g + 1) * hw] = dqkv_ref[g, :, hw:2 * hw]
        y_ref[:, g * hw:(g + 1) * hw] = dqkv_ref[g, :, 2 * hw:3 * hw]
    grad = dot(y_ref[...], wqkv_ref[...], NT) * gain_ref[...]
    center, inv = centered(rows_ref[0].astype(F32))
    unit = center * inv
    mean = jnp.mean(grad, axis=-1, keepdims=True)
    along = jnp.mean(grad * unit, axis=-1, keepdims=True)
    pulled = inv * (grad - mean - unit * along)
    out_ref[...] = (up_ref[...].astype(F32) + pulled).astype(BF16)


def call(kernel, out_shape, operands, scratch=(), smem=0, cost=None, name=None, picked=None):
    specs = [pl.BlockSpec(memory_space=pltpu.SMEM)] * smem
    specs += [pl.BlockSpec(memory_space=pltpu.VMEM)] * (len(operands) - smem)
    kwargs = dict(
        out_shape=jax.ShapeDtypeStruct(out_shape, BF16),
        cost_estimate=pl.CostEstimate(flops=cost[0], bytes_accessed=cost[1], transcendentals=0),
        compiler_params=pltpu.CompilerParams(vmem_limit_bytes=VMEM_LIMIT),
        name=name,
    )
    if picked is None:
        return pl.pallas_call(
            kernel,
            in_specs=specs,
            out_specs=pl.BlockSpec(memory_space=pltpu.VMEM),
            scratch_shapes=list(scratch),
            **kwargs,
        )(*operands)

    def whole(shape):
        return pl.BlockSpec(shape, lambda i, pick: (0,) * len(shape))

    specs = [whole(o.shape) for o in operands[1:]]
    stash = operands[picked]
    specs[picked - 1] = pl.BlockSpec((1,) + stash.shape[1:], lambda i, pick: (pick[0], 0, 0))
    return pl.pallas_call(
        kernel,
        grid_spec=pltpu.PrefetchScalarGridSpec(
            num_scalar_prefetch=1,
            grid=(1,),
            in_specs=specs,
            out_specs=whole(out_shape),
            scratch_shapes=list(scratch),
        ),
        **kwargs,
    )(*operands)


def places(owners, groups):
    count = owners.shape[0]
    key = owners * count + jnp.arange(count, dtype=jnp.int32)
    pos = jnp.sum((key[None, :] < key[:, None]).astype(jnp.int32), axis=1)
    bounds = jnp.arange(groups + 1, dtype=jnp.int32)
    start = jnp.sum((owners[None, :] < bounds[:, None]).astype(jnp.int32), axis=1)
    return pos, start


def swap(value):
    return lax.all_to_all(value, "space", split_axis=0, concat_axis=0, tiled=True)


def on_device(
    act_in, stash, plan, grad_in, fwd_owner, stash_owner, ln_gain, qkv_weight, proj_weight
):
    groups = lax.axis_size("space")
    rows_in = act_in[0]
    rows, width = rows_in.shape
    head_dim = width // HEADS
    hw = width // groups
    blk = rows // groups
    heads = hw // head_dim
    total = groups * rows
    span = heads * QT
    w_qkv = qkv_weight[0]
    w_proj = proj_weight[0]
    stored = stash[0]
    upstream = grad_in[0]
    stored_owners = lax.dynamic_index_in_dim(stash_owner[0], plan[0], 0, keepdims=False)
    mine = jnp.stack([fwd_owner[0][::blk], stored_owners[::blk]])
    owners = lax.all_gather(mine, "space", axis=0)
    pos, start = places(owners[:, 0].reshape(-1), groups)
    pos_b, start_b = places(owners[:, 1].reshape(-1), groups)

    sent = call(
        functools.partial(project_kernel, groups, hw),
        (groups, rows, 3 * hw),
        (rows_in, ln_gain, w_qkv),
        [pltpu.VMEM((rows, 3 * width), BF16)],
        cost=(6 * rows * width * width, 5 * 1024 * 1024),
        name="project",
    )
    sent_b = call(
        functools.partial(project_grad_kernel, groups, hw),
        (groups, rows, 4 * hw),
        (plan, stored, upstream, ln_gain, w_qkv, w_proj),
        [pltpu.VMEM((rows, 3 * width), BF16), pltpu.VMEM((rows, width), BF16)],
        cost=(8 * rows * width * width, 6 * 1024 * 1024),
        name="project_grad",
        picked=1,
    )
    got = swap(sent)
    got_b = swap(sent_b)
    attended = call(
        functools.partial(attend_kernel, groups, blk, hw, head_dim),
        (groups, rows, hw),
        (pos, start, got),
        [
            pltpu.VMEM((total + KT, 2 * hw), BF16),
            pltpu.VMEM((total + KT, hw), BF16),
            pltpu.VMEM((total + KT, hw), BF16),
            pltpu.VMEM((2 * hw, PATCH), BF16),
            pltpu.VMEM((PATCH, span), BF16),
        ],
        smem=2,
        cost=(10_000_000_000, 3 * 1024 * 1024),
        name="attend",
    )
    ret = swap(attended)
    grads = call(
        functools.partial(attend_grad_kernel, groups, blk, hw, head_dim),
        (groups, rows, 3 * hw),
        (pos_b, start_b, got_b),
        [
            pltpu.VMEM((total + KT, 2 * hw), BF16),
            pltpu.VMEM((total + KT, 2 * hw), BF16),
            pltpu.VMEM((total + KT, hw), BF16),
            pltpu.VMEM((total + KT, 2 * hw), BF16),
            pltpu.VMEM((2 * hw, PATCH), BF16),
            pltpu.VMEM((PATCH, 2 * span), BF16),
            pltpu.VMEM((PATCH, 2 * hw), F32),
        ],
        smem=2,
        cost=(30_000_000_000, 4 * 1024 * 1024),
        name="attend_grad",
    )
    ret_grads = swap(grads)
    mixed = call(
        functools.partial(mix_kernel, groups, hw),
        (rows, width),
        (ret, rows_in, w_proj),
        [pltpu.VMEM((rows, width), BF16)],
        cost=(2 * rows * width * width, 2 * 1024 * 1024),
        name="mix",
    )
    act_out = passed_along(mixed[None], "section", 1)
    input_grad = call(
        functools.partial(input_grad_kernel, groups, hw),
        (rows, width),
        (plan, ret_grads, stored, upstream, ln_gain, w_qkv),
        [pltpu.VMEM((rows, 3 * width), BF16)],
        cost=(6 * rows * width * width, 5 * 1024 * 1024),
        name="input_grad",
        picked=2,
    )
    grad_out = passed_along(input_grad[None], "section", -1)
    return (act_out, grad_out)


def solution(mesh):
    in_specs = (
        P("section", "space", None),
        P("section", None, "space", None),
        P("section"),
        P("section", "space", None),
        P("section", "space"),
        P("section", None, "space"),
        P("section", None),
        P("section", None, None),
        P("section", None, None),
    )
    out_specs = (P("section", "space", None), P("section", "space", None))
    return jax.shard_map(
        on_device, mesh=mesh, in_specs=in_specs, out_specs=out_specs, check_vma=False
    )
```

```python
import functools
import math

import jax
import jax.numpy as jnp
from jax import lax
from jax.experimental import pallas as pl
from jax.experimental.pallas import tpu as pltpu
from jax.sharding import PartitionSpec as P

HEADS = 32
EPS = 1e-05
NEG = -1e30
QT = 128
KT = 256
PATCH = 1024
VMEM_LIMIT = 56 * 1024 * 1024
F32 = jnp.float32
BF16 = jnp.bfloat16
NT = (((1,), (1,)), ((), ()))
NN = (((1,), (0,)), ((), ()))


def dot(a, b, dims=NN):
    return lax.dot_general(a, b, dims, preferred_element_type=F32)


def passed_along(value, axis, by):
    size = lax.axis_size(axis)
    pairs = [(i, i + by) for i in range(size) if 0 <= i + by < size]
    return lax.ppermute(value, axis, pairs)


def centered(values):
    center = values - jnp.mean(values, axis=-1, keepdims=True)
    spread = jnp.mean(center * center, axis=-1, keepdims=True)
    return center, lax.rsqrt(spread + EPS)


def spread(groups, hw, y_ref, out_ref):
    rows, width = y_ref.shape[0], y_ref.shape[1] // 3
    for g in range(groups):
        low = g * hw
        out_ref[g, 0:rows, 0:hw] = y_ref[:, width + low:width + low + hw]
        out_ref[g, 0:rows, hw:2 * hw] = y_ref[:, 2 * width + low:2 * width + low + hw]


def project_kernel(groups, hw, rows_ref, gain_ref, wqkv_ref, out_ref, y_ref):
    rows = rows_ref.shape[0]
    half = rows // 2
    center, inv = centered(rows_ref[...].astype(F32))
    normed = (center * inv * gain_ref[...]).astype(BF16)
    y_ref[...] = dot(normed, wqkv_ref[...]).astype(BF16)
    spread(groups, hw, y_ref, out_ref)
    for g in range(groups):
        out_ref[g, rows:rows + half, 0:hw] = y_ref[0:half, g * hw:(g + 1) * hw]
        out_ref[g, rows:rows + half, hw:2 * hw] = y_ref[half:rows, g * hw:(g + 1) * hw]


def project_grad_kernel(
    groups,
    hw,
    pick_ref,
    rows_ref,
    up_ref,
    gain_ref,
    wqkv_ref,
    wproj_ref,
    owners_ref,
    out_ref,
    y_ref,
    d_ref,
):
    rows = up_ref.shape[0]
    center, inv = centered(rows_ref[0].astype(F32))
    normed = (center * inv * gain_ref[...]).astype(BF16)
    y_ref[...] = dot(normed, wqkv_ref[...]).astype(BF16)
    d_ref[...] = dot(up_ref[...], wproj_ref[...], NT).astype(BF16)
    spread(groups, hw, y_ref, out_ref)
    for g in range(groups):
        out_ref[g, rows:2 * rows, 0:hw] = y_ref[:, g * hw:(g + 1) * hw]
        out_ref[g, rows:2 * rows, hw:2 * hw] = d_ref[:, g * hw:(g + 1) * hw]
        out_ref[g, 2 * rows:, :] = owners_ref[...]


def stacked(tile, head_dim, heads, offset):
    lane = lax.broadcasted_iota(jnp.int32, tile.shape, 1)
    zero = jnp.zeros_like(tile)
    parts = []
    for h in range(heads):
        low = offset + h * head_dim
        parts.append(jnp.where((lane >= low) & (lane < low + head_dim), tile, zero))
    return jnp.concatenate(parts, axis=0)


def own_blocks(wide, head_dim, heads):
    picked = [
        wide[h * head_dim:(h + 1) * head_dim, h * QT:(h + 1) * QT] for h in range(heads)
    ]
    return jnp.concatenate(picked, axis=0).T


def each_block(groups, per_group, blk, body, first=0, count=None):
    count = per_group if count is None else count

    def step(b, carry):
        g, j = b // count, first + b % count
        body(g * per_group + j, g, pl.multiple_of(j * blk, blk))
        return carry

    lax.fori_loop(0, groups * count, step, 0)


def each_patch(which, groups, blk, at_ref, small, body):
    n_blocks = at_ref.shape[1] - groups - 1

    def step(o, carry):
        first = at_ref[which, n_blocks + o]
        live = (at_ref[which, n_blocks + o + 1] - first) * blk
        base = pl.multiple_of(first * blk, blk)
        for slots in range(KT, PATCH + 1, KT):
            fits = (live > slots - KT) & (live <= slots)

            @pl.when(fits & small)
            def _():
                body(slots, base, live, False)

            @pl.when(fits & jnp.logical_not(small))
            def _():
                body(slots, base, live, True)

        return carry

    lax.fori_loop(0, groups, step, 0)


def largest_norm(tiles, hw, head_dim):
    lanes = 2 * hw
    col = lax.broadcasted_iota(jnp.int32, (lanes, 128), 0)
    head = lax.broadcasted_iota(jnp.int32, (lanes, 128), 1)
    pick = ((col // head_dim == head) & (col < hw)).astype(BF16)
    best = None
    for tile in tiles:
        values = tile.astype(F32)
        norm = jnp.max(dot((values * values).astype(BF16), pick), axis=0, keepdims=True)
        best = norm if best is None else jnp.maximum(best, norm)
    return jnp.max(best)


def probs_of(scores, live, shifted):
    tiles = list(scores)
    low = (len(tiles) - 1) * KT
    row = lax.broadcasted_iota(jnp.int32, tiles[-1].shape, 0) + low
    tiles[-1] = jnp.where(row < live, tiles[-1], NEG)
    if shifted:
        top = functools.reduce(jnp.maximum, [jnp.max(t, axis=0, keepdims=True) for t in tiles])
        tiles = [t - top for t in tiles]
    expd = [jnp.exp(t) for t in tiles]
    total = functools.reduce(jnp.add, [jnp.sum(t, axis=0, keepdims=True) for t in expd])
    inv = 1.0 / total
    return [t * inv for t in expd]


def attend_kernel(
    groups, blk, hw, head_dim, at_ref, x_ref, out_ref, kv, qs, res, kvt, pb
):
    heads = hw // head_dim
    scale = 1.0 / math.sqrt(head_dim)
    rows = out_ref.shape[1] * 2
    half = rows // 2
    per_group = rows // blk
    total = groups * rows

    kv[pl.ds(total, KT), :] = jnp.zeros((KT, 2 * hw), BF16)
    qs[pl.ds(total, KT), :] = jnp.zeros((KT, 2 * hw), BF16)
    qs[0:total, hw:2 * hw] = jnp.zeros((total, hw), BF16)

    for side in range(2):
        def place(b, g, r):
            to = pl.multiple_of(at_ref[0, b] * blk, blk)
            kv[pl.ds(to, blk), :] = x_ref[g, pl.ds(r, blk), :]
            from_row = pl.multiple_of(r + (rows - side * half), blk)
            qs[pl.ds(to, blk), 0:hw] = x_ref[g, pl.ds(from_row, blk), side * hw:(side + 1) * hw]

        each_block(groups, per_group, blk, place, side * per_group // 2, per_group // 2)

    key_norm = largest_norm([kv[t:t + rows, :] for t in range(0, total, rows)], hw, head_dim)
    query_norm = largest_norm([qs[t:t + rows, :] for t in range(0, total, rows)], hw, head_dim)
    small = key_norm * query_norm * (scale * scale) < 2500.0

    def patch(slots, base, live, shifted):
        kvt[:, 0:slots] = kv[pl.ds(base, slots), :].T
        pb[0:slots, :] = jnp.zeros((slots, heads * QT), BF16)

        def flush(c):
            at = pl.multiple_of(base + c * QT, blk)
            wide = dot(kvt[hw:2 * hw, 0:slots], pb[0:slots, :])
            res[pl.ds(at, QT), :] = own_blocks(wide, head_dim, heads).astype(BF16)

        def chunk(c, carry):
            at = pl.multiple_of(base + c * QT, blk)
            q = (qs[pl.ds(at, QT), :].astype(F32) * scale).astype(BF16)
            q_st = stacked(q, head_dim, heads, 0)
            scores = [
                dot(kv[pl.ds(pl.multiple_of(base + t, blk), KT), :], q_st, NT)
                for t in range(0, slots, KT)
            ]
            flush(jnp.maximum(c - 1, 0))
            for t, p in enumerate(probs_of(scores, live, shifted)):
                pb[t * KT:(t + 1) * KT, :] = p.astype(BF16)
            return carry

        chunks = (live + QT - 1) // QT
        lax.fori_loop(0, chunks, chunk, 0)
        flush(chunks - 1)

    each_patch(0, groups, blk, at_ref, small, patch)

    for side in range(2):
        def back(b, g, r):
            at = pl.multiple_of(at_ref[0, b] * blk, blk)
            to = pl.multiple_of(r - side * half, blk)
            out_ref[g, pl.ds(to, blk), side * hw:(side + 1) * hw] = res[pl.ds(at, blk), :]

        each_block(groups, per_group, blk, back, side * per_group // 2, per_group // 2)


def attend_grad_kernel(
    groups, blk, hw, head_dim, at_ref, x_ref, out_ref, kv, qd, dq, dkv, kvt, both, acc, right
):
    heads = hw // head_dim
    scale = 1.0 / math.sqrt(head_dim)
    rows = out_ref.shape[1] * 2 // 3
    half = rows // 2
    per_group = rows // blk
    total = groups * rows
    span = heads * QT

    kv[pl.ds(total, KT), :] = jnp.zeros((KT, 2 * hw), BF16)
    qd[pl.ds(total, KT), :] = jnp.zeros((KT, 2 * hw), BF16)

    def place(b, g, r):
        to = pl.multiple_of(at_ref[1, b] * blk, blk)
        kv[pl.ds(to, blk), :] = x_ref[g, pl.ds(r, blk), :]
        qd[pl.ds(to, blk), :] = x_ref[g, pl.ds(pl.multiple_of(r + rows, blk), blk), :]

    each_block(groups, per_group, blk, place)

    key_norm = largest_norm([kv[t:t + rows, :] for t in range(0, total, rows)], hw, head_dim)
    query_norm = largest_norm([qd[t:t + rows, :] for t in range(0, total, rows)], hw, head_dim)
    small = key_norm * query_norm * (scale * scale) < 2500.0

    def patch(slots, base, live, shifted):
        kvt[:, 0:slots] = kv[pl.ds(base, slots), :].T
        acc[0:slots, :] = jnp.zeros((slots, 2 * hw), F32)
        both[0:slots, :] = jnp.zeros((slots, 2 * span), BF16)
        right[...] = jnp.zeros(right.shape, BF16)

        def flush(c):
            at = pl.multiple_of(base + c * QT, blk)
            acc[0:slots, :] += dot(both[0:slots, :], right[...])
            wide = dot(kvt[0:hw, 0:slots], both[0:slots, 0:span]) * scale
            dq[pl.ds(at, QT), :] = own_blocks(wide, head_dim, heads).astype(BF16)

        def chunk(c, carry):
            at = pl.multiple_of(base + c * QT, blk)
            tile = qd[pl.ds(at, QT), :]
            q_st = stacked((tile.astype(F32) * scale).astype(BF16), head_dim, heads, 0)
            row = lax.broadcasted_iota(jnp.int32, tile.shape, 0) + c * QT
            d_st = stacked(jnp.where(row < live, tile, jnp.zeros_like(tile)), head_dim, heads, hw)
            keys = [
                kv[pl.ds(pl.multiple_of(base + t, blk), KT), :] for t in range(0, slots, KT)
            ]
            scores = [dot(k, q_st, NT) for k in keys]
            grads = [dot(k, d_st, NT) for k in keys]
            flush(jnp.maximum(c - 1, 0))
            right[0:span, :] = q_st
            right[span:2 * span, :] = d_st
            probs = probs_of(scores, live, shifted)
            delta = functools.reduce(
                jnp.add, [jnp.sum(p * g, axis=0, keepdims=True) for p, g in zip(probs, grads)]
            )
            for t, (p, g) in enumerate(zip(probs, grads)):
                both[t * KT:(t + 1) * KT, 0:span] = (p * (g - delta)).astype(BF16)
                both[t * KT:(t + 1) * KT, span:2 * span] = p.astype(BF16)
            return carry

        chunks = (live + QT - 1) // QT
        lax.fori_loop(0, chunks, chunk, 0)
        flush(chunks - 1)
        dkv[pl.ds(base, slots), :] = acc[0:slots, :].astype(BF16)

    each_patch(1, groups, blk, at_ref, small, patch)

    for side in range(2):
        def back(b, g, r):
            at = pl.multiple_of(at_ref[1, b] * blk, blk)
            out_ref[g, pl.ds(r, blk), :] = dkv[pl.ds(at, blk), :]
            to = pl.multiple_of(r + (rows - side * half), blk)
            out_ref[g, pl.ds(to, blk), side * hw:(side + 1) * hw] = dq[pl.ds(at, blk), :]

        each_block(groups, per_group, blk, back, side * per_group // 2, per_group // 2)


def mix_kernel(groups, hw, att_ref, rows_ref, wproj_ref, out_ref, a_ref):
    half = a_ref.shape[0] // 2
    for g in range(groups):
        a_ref[0:half, g * hw:(g + 1) * hw] = att_ref[g, :, 0:hw]
        a_ref[half:2 * half, g * hw:(g + 1) * hw] = att_ref[g, :, hw:2 * hw]
    mixed = rows_ref[...].astype(F32) + dot(a_ref[...], wproj_ref[...])
    out_ref[...] = mixed.astype(BF16)


def input_grad_kernel(
    groups, hw, pick_ref, dqkv_ref, rows_ref, up_ref, gain_ref, wqkv_ref, out_ref, y_ref
):
    rows, width = up_ref.shape
    half = rows // 2
    for g in range(groups):
        low = g * hw
        y_ref[:, width + low:width + low + hw] = dqkv_ref[g, 0:rows, 0:hw]
        y_ref[:, 2 * width + low:2 * width + low + hw] = dqkv_ref[g, 0:rows, hw:2 * hw]
        y_ref[0:half, low:low + hw] = dqkv_ref[g, rows:rows + half, 0:hw]
        y_ref[half:rows, low:low + hw] = dqkv_ref[g, rows:rows + half, hw:2 * hw]
    grad = dot(y_ref[...], wqkv_ref[...], NT) * gain_ref[...]
    center, inv = centered(rows_ref[0].astype(F32))
    unit = center * inv
    mean = jnp.mean(grad, axis=-1, keepdims=True)
    along = jnp.mean(grad * unit, axis=-1, keepdims=True)
    pulled = inv * (grad - mean - unit * along)
    out_ref[...] = (up_ref[...].astype(F32) + pulled).astype(BF16)


def call(kernel, out_shape, operands, scratch=(), smem=0, cost=None, name=None, picked=None):
    specs = [pl.BlockSpec(memory_space=pltpu.SMEM)] * smem
    specs += [pl.BlockSpec(memory_space=pltpu.VMEM)] * (len(operands) - smem)
    kwargs = dict(
        out_shape=jax.ShapeDtypeStruct(out_shape, BF16),
        cost_estimate=pl.CostEstimate(flops=cost[0], bytes_accessed=cost[1], transcendentals=0),
        compiler_params=pltpu.CompilerParams(vmem_limit_bytes=VMEM_LIMIT),
        name=name,
    )
    if picked is None:
        return pl.pallas_call(
            kernel,
            in_specs=specs,
            out_specs=pl.BlockSpec(memory_space=pltpu.VMEM),
            scratch_shapes=list(scratch),
            **kwargs,
        )(*operands)

    def whole(shape):
        return pl.BlockSpec(shape, lambda i, pick: (0,) * len(shape))

    specs = [whole(o.shape) for o in operands[1:]]
    stash = operands[picked]
    specs[picked - 1] = pl.BlockSpec((1,) + stash.shape[1:], lambda i, pick: (pick[0], 0, 0))
    return pl.pallas_call(
        kernel,
        grid_spec=pltpu.PrefetchScalarGridSpec(
            num_scalar_prefetch=1,
            grid=(1,),
            in_specs=specs,
            out_specs=whole(out_shape),
            scratch_shapes=list(scratch),
        ),
        **kwargs,
    )(*operands)


def places(owners, groups):
    count = owners.shape[1]
    key = owners * count + jnp.arange(count, dtype=jnp.int32)
    bounds = jnp.broadcast_to(jnp.arange(groups + 1, dtype=jnp.int32) * count, (2, groups + 1))
    marks = jnp.concatenate([key, bounds], axis=1)
    return jnp.sum((key[:, None, :] < marks[:, :, None]).astype(jnp.int32), axis=2)


def swap(value):
    return lax.all_to_all(value, "space", split_axis=0, concat_axis=0, tiled=True)


def on_device(
    act_in, stash, plan, grad_in, fwd_owner, stash_owner, ln_gain, qkv_weight, proj_weight
):
    groups = lax.axis_size("space")
    rows_in = act_in[0]
    rows, width = rows_in.shape
    head_dim = width // HEADS
    hw = width // groups
    blk = rows // groups
    heads = hw // head_dim
    total = groups * rows
    span = heads * QT
    w_qkv = qkv_weight[0]
    w_proj = proj_weight[0]
    stored = stash[0]
    upstream = grad_in[0]
    stored_owners = lax.dynamic_index_in_dim(stash_owner[0], plan[0], 0, keepdims=False)
    mine = jnp.stack([fwd_owner[0], stored_owners]).reshape(2, groups, blk)[:, :, 0]
    owner_rows = jnp.pad(mine.astype(BF16), ((0, 14), (0, 2 * hw - groups)))

    sent_b = call(
        functools.partial(project_grad_kernel, groups, hw),
        (groups, 2 * rows + 16, 2 * hw),
        (plan, stored, upstream, ln_gain, w_qkv, w_proj, owner_rows),
        [pltpu.VMEM((rows, 3 * width), BF16), pltpu.VMEM((rows, width), BF16)],
        cost=(8 * rows * width * width, 6 * 1024 * 1024),
        name="project_grad",
        picked=1,
    )
    got_b = swap(sent_b)
    sent = call(
        functools.partial(project_kernel, groups, hw),
        (groups, 3 * rows // 2, 2 * hw),
        (rows_in, ln_gain, w_qkv),
        [pltpu.VMEM((rows, 3 * width), BF16)],
        cost=(6 * rows * width * width, 5 * 1024 * 1024),
        name="project",
    )
    got = swap(sent)
    owners = got_b[:, 2 * rows:2 * rows + 2, 0:groups].astype(jnp.int32)
    at = places(owners.transpose(1, 0, 2).reshape(2, groups * groups), groups)
    grads = call(
        functools.partial(attend_grad_kernel, groups, blk, hw, head_dim),
        (groups, 3 * rows // 2, 2 * hw),
        (at, got_b),
        [
            pltpu.VMEM((total + KT, 2 * hw), BF16),
            pltpu.VMEM((total + KT, 2 * hw), BF16),
            pltpu.VMEM((total + KT, hw), BF16),
            pltpu.VMEM((total + KT, 2 * hw), BF16),
            pltpu.VMEM((2 * hw, PATCH), BF16),
            pltpu.VMEM((PATCH, 2 * span), BF16),
            pltpu.VMEM((PATCH, 2 * hw), F32),
            pltpu.VMEM((2 * span, 2 * hw), BF16),
        ],
        smem=1,
        cost=(30_000_000_000, 4 * 1024 * 1024),
        name="attend_grad",
    )
    grads, got = lax.optimization_barrier((grads, got))
    ret_grads = swap(grads)
    attended = call(
        functools.partial(attend_kernel, groups, blk, hw, head_dim),
        (groups, rows // 2, 2 * hw),
        (at, got),
        [
            pltpu.VMEM((total + KT, 2 * hw), BF16),
            pltpu.VMEM((total + KT, 2 * hw), BF16),
            pltpu.VMEM((total + KT, hw), BF16),
            pltpu.VMEM((2 * hw, PATCH), BF16),
            pltpu.VMEM((PATCH, span), BF16),
        ],
        smem=1,
        cost=(20_000_000_000, 3 * 1024 * 1024),
        name="attend",
    )
    ret_grads, attended = lax.optimization_barrier((ret_grads, attended))
    ret = swap(attended)
    input_grad = call(
        functools.partial(input_grad_kernel, groups, hw),
        (rows, width),
        (plan, ret_grads, stored, upstream, ln_gain, w_qkv),
        [pltpu.VMEM((rows, 3 * width), BF16)],
        cost=(6 * rows * width * width, 5 * 1024 * 1024),
        name="input_grad",
        picked=2,
    )
    grad_out = passed_along(input_grad[None], "section", -1)
    mixed = call(
        functools.partial(mix_kernel, groups, hw),
        (rows, width),
        (ret, rows_in, w_proj),
        [pltpu.VMEM((rows, width), BF16)],
        cost=(2 * rows * width * width, 2 * 1024 * 1024),
        name="mix",
    )
    act_out = passed_along(mixed[None], "section", 1)
    return (act_out, grad_out)


def solution(mesh):
    in_specs = (
        P("section", "space", None),
        P("section", None, "space", None),
        P("section"),
        P("section", "space", None),
        P("section", "space"),
        P("section", None, "space"),
        P("section", None),
        P("section", None, None),
        P("section", None, None),
    )
    out_specs = (P("section", "space", None), P("section", "space", None))
    return jax.shard_map(
        on_device, mesh=mesh, in_specs=in_specs, out_specs=out_specs, check_vma=False
    )
```

```python
import functools
import math

import jax
import jax.numpy as jnp
from jax import lax
from jax.experimental import pallas as pl
from jax.experimental.pallas import tpu as pltpu
from jax.sharding import PartitionSpec as P

HEADS = 32
EPS = 1e-05
NEG = -1e30
QT = 128
KT = 256
PATCH = 1024
VMEM_LIMIT = 56 * 1024 * 1024
F32 = jnp.float32
BF16 = jnp.bfloat16
NT = (((1,), (1,)), ((), ()))
NN = (((1,), (0,)), ((), ()))


def dot(a, b, dims=NN):
    return lax.dot_general(a, b, dims, preferred_element_type=F32)


def passed_along(value, axis, by):
    size = lax.axis_size(axis)
    pairs = [(i, i + by) for i in range(size) if 0 <= i + by < size]
    return lax.ppermute(value, axis, pairs)


def centered(values):
    center = values - jnp.mean(values, axis=-1, keepdims=True)
    spread = jnp.mean(center * center, axis=-1, keepdims=True)
    return center, lax.rsqrt(spread + EPS)


def spread(groups, hw, y_ref, out_ref):
    rows, width = y_ref.shape[0], y_ref.shape[1] // 3
    for g in range(groups):
        low = g * hw
        out_ref[g, 0:rows, 0:hw] = y_ref[:, width + low:width + low + hw]
        out_ref[g, 0:rows, hw:2 * hw] = y_ref[:, 2 * width + low:2 * width + low + hw]


def project_kernel(groups, hw, rows_ref, gain_ref, wqkv_ref, out_ref, y_ref):
    rows = rows_ref.shape[0]
    half = rows // 2
    center, inv = centered(rows_ref[...].astype(F32))
    normed = (center * inv * gain_ref[...]).astype(BF16)
    y_ref[...] = dot(normed, wqkv_ref[...]).astype(BF16)
    spread(groups, hw, y_ref, out_ref)
    for g in range(groups):
        out_ref[g, rows:rows + half, 0:hw] = y_ref[0:half, g * hw:(g + 1) * hw]
        out_ref[g, rows:rows + half, hw:2 * hw] = y_ref[half:rows, g * hw:(g + 1) * hw]


def project_grad_kernel(
    groups,
    hw,
    pick_ref,
    rows_ref,
    up_ref,
    gain_ref,
    wqkv_ref,
    wproj_ref,
    owners_ref,
    out_ref,
    y_ref,
    d_ref,
):
    rows = up_ref.shape[0]
    center, inv = centered(rows_ref[0].astype(F32))
    normed = (center * inv * gain_ref[...]).astype(BF16)
    y_ref[...] = dot(normed, wqkv_ref[...]).astype(BF16)
    d_ref[...] = dot(up_ref[...], wproj_ref[...], NT).astype(BF16)
    spread(groups, hw, y_ref, out_ref)
    for g in range(groups):
        out_ref[g, rows:2 * rows, 0:hw] = y_ref[:, g * hw:(g + 1) * hw]
        out_ref[g, rows:2 * rows, hw:2 * hw] = d_ref[:, g * hw:(g + 1) * hw]
        out_ref[g, 2 * rows:, :] = owners_ref[...]


def stacked(tile, head_dim, heads, offset):
    lane = lax.broadcasted_iota(jnp.int32, tile.shape, 1)
    zero = jnp.zeros_like(tile)
    parts = []
    for h in range(heads):
        low = offset + h * head_dim
        parts.append(jnp.where((lane >= low) & (lane < low + head_dim), tile, zero))
    return jnp.concatenate(parts, axis=0)


def stacked_columns(tile_t, head_dim, heads, offset):
    row = lax.broadcasted_iota(jnp.int32, tile_t.shape, 0)
    parts = []
    for h in range(heads):
        low = offset + h * head_dim
        parts.append(jnp.where((row >= low) & (row < low + head_dim), tile_t, 0.0))
    return jnp.concatenate(parts, axis=1).astype(BF16)


def own_blocks(wide, head_dim, heads):
    picked = [
        wide[h * head_dim:(h + 1) * head_dim, h * QT:(h + 1) * QT] for h in range(heads)
    ]
    return jnp.concatenate(picked, axis=0).T


def each_block(groups, per_group, blk, body, first=0, count=None):
    count = per_group if count is None else count

    def step(g, carry):
        for j in range(first, first + count):
            body(g * per_group + j, g, j * blk)
        return carry

    lax.fori_loop(0, groups, step, 0)


def each_patch(which, groups, blk, at_ref, small, body):
    n_blocks = at_ref.shape[1] - groups - 1

    def step(o, carry):
        first = at_ref[which, n_blocks + o]
        live = (at_ref[which, n_blocks + o + 1] - first) * blk
        base = pl.multiple_of(first * blk, blk)
        for slots in range(KT, PATCH + 1, KT):
            fits = (live > slots - KT) & (live <= slots)

            @pl.when(fits & small)
            def _():
                body(slots, base, live, False)

            @pl.when(fits & jnp.logical_not(small))
            def _():
                body(slots, base, live, True)

        return carry

    lax.fori_loop(0, groups, step, 0)


def largest_norm(tiles, hw, head_dim):
    lanes = 2 * hw
    col = lax.broadcasted_iota(jnp.int32, (lanes, 128), 0)
    head = lax.broadcasted_iota(jnp.int32, (lanes, 128), 1)
    pick = ((col // head_dim == head) & (col < hw)).astype(BF16)
    best = None
    for tile in tiles:
        values = tile.astype(F32)
        norm = jnp.max(dot((values * values).astype(BF16), pick), axis=0, keepdims=True)
        best = norm if best is None else jnp.maximum(best, norm)
    return jnp.max(best)


def probs_of(scores, live, shifted):
    tiles = list(scores)
    low = (len(tiles) - 1) * KT
    row = lax.broadcasted_iota(jnp.int32, tiles[-1].shape, 0) + low
    tiles[-1] = jnp.where(row < live, tiles[-1], NEG)
    if shifted:
        top = functools.reduce(jnp.maximum, [jnp.max(t, axis=0, keepdims=True) for t in tiles])
        tiles = [t - top for t in tiles]
    expd = [jnp.exp(t) for t in tiles]
    total = functools.reduce(jnp.add, [jnp.sum(t, axis=0, keepdims=True) for t in expd])
    inv = 1.0 / total
    return [t * inv for t in expd]


def attend_kernel(
    groups, blk, hw, head_dim, at_ref, x_ref, out_ref, kv, qs, res, kvt, pb
):
    heads = hw // head_dim
    scale = 1.0 / math.sqrt(head_dim)
    rows = out_ref.shape[1] * 2
    half = rows // 2
    per_group = rows // blk
    total = groups * rows

    kv[pl.ds(total, KT), :] = jnp.zeros((KT, 2 * hw), BF16)
    qs[pl.ds(total, KT), :] = jnp.zeros((KT, 2 * hw), BF16)
    qs[0:total, hw:2 * hw] = jnp.zeros((total, hw), BF16)

    for side in range(2):
        def place(b, g, r):
            to = pl.multiple_of(at_ref[0, b] * blk, blk)
            kv[pl.ds(to, blk), :] = x_ref[g, pl.ds(r, blk), :]
            from_row = r + rows - side * half
            qs[pl.ds(to, blk), 0:hw] = x_ref[g, pl.ds(from_row, blk), side * hw:(side + 1) * hw]

        each_block(groups, per_group, blk, place, side * per_group // 2, per_group // 2)

    key_norm = largest_norm([kv[t:t + rows, :] for t in range(0, total, rows)], hw, head_dim)
    query_norm = largest_norm([qs[t:t + rows, :] for t in range(0, total, rows)], hw, head_dim)
    small = key_norm * query_norm * (scale * scale) < 2500.0

    def patch(slots, base, live, shifted):
        kvt[:, 0:slots] = kv[pl.ds(base, slots), :].T
        pb[0:slots, :] = jnp.zeros((slots, heads * QT), BF16)

        def flush(c):
            at = pl.multiple_of(base + c * QT, blk)
            wide = dot(kvt[hw:2 * hw, 0:slots], pb[0:slots, :])
            res[pl.ds(at, QT), :] = own_blocks(wide, head_dim, heads).astype(BF16)

        def chunk(c, carry):
            at = pl.multiple_of(base + c * QT, blk)
            q = qs[pl.ds(at, QT), :].astype(F32) * scale
            q_cols = stacked_columns(q.T, head_dim, heads, 0)
            scores = [
                dot(kv[pl.ds(pl.multiple_of(base + t, blk), KT), :], q_cols)
                for t in range(0, slots, KT)
            ]
            flush(jnp.maximum(c - 1, 0))
            for t, p in enumerate(probs_of(scores, live, shifted)):
                pb[t * KT:(t + 1) * KT, :] = p.astype(BF16)
            return carry

        chunks = (live + QT - 1) // QT
        lax.fori_loop(0, chunks, chunk, 0)
        flush(chunks - 1)

    each_patch(0, groups, blk, at_ref, small, patch)

    for side in range(2):
        def back(b, g, r):
            at = pl.multiple_of(at_ref[0, b] * blk, blk)
            to = r - side * half
            out_ref[g, pl.ds(to, blk), side * hw:(side + 1) * hw] = res[pl.ds(at, blk), :]

        each_block(groups, per_group, blk, back, side * per_group // 2, per_group // 2)


def attend_grad_kernel(
    groups, blk, hw, head_dim, at_ref, x_ref, out_ref, kv, qd, dq, dkv, kvt, both, acc, right
):
    heads = hw // head_dim
    scale = 1.0 / math.sqrt(head_dim)
    rows = out_ref.shape[1] * 2 // 3
    half = rows // 2
    per_group = rows // blk
    total = groups * rows
    span = heads * QT

    kv[pl.ds(total, KT), :] = jnp.zeros((KT, 2 * hw), BF16)
    qd[pl.ds(total, KT), :] = jnp.zeros((KT, 2 * hw), BF16)

    def place(b, g, r):
        to = pl.multiple_of(at_ref[1, b] * blk, blk)
        kv[pl.ds(to, blk), :] = x_ref[g, pl.ds(r, blk), :]
        qd[pl.ds(to, blk), :] = x_ref[g, pl.ds(r + rows, blk), :]

    each_block(groups, per_group, blk, place)

    key_norm = largest_norm([kv[t:t + rows, :] for t in range(0, total, rows)], hw, head_dim)
    query_norm = largest_norm([qd[t:t + rows, :] for t in range(0, total, rows)], hw, head_dim)
    small = key_norm * query_norm * (scale * scale) < 2500.0

    def patch(slots, base, live, shifted):
        kvt[:, 0:slots] = kv[pl.ds(base, slots), :].T
        acc[0:slots, :] = jnp.zeros((slots, 2 * hw), F32)
        both[0:slots, :] = jnp.zeros((slots, 2 * span), BF16)
        right[...] = jnp.zeros(right.shape, BF16)

        def flush(c):
            at = pl.multiple_of(base + c * QT, blk)
            acc[0:slots, :] += dot(both[0:slots, :], right[...])
            wide = dot(kvt[0:hw, 0:slots], both[0:slots, 0:span]) * scale
            dq[pl.ds(at, QT), :] = own_blocks(wide, head_dim, heads).astype(BF16)

        def chunk(c, carry):
            at = pl.multiple_of(base + c * QT, blk)
            tile = qd[pl.ds(at, QT), :]
            q_st = stacked((tile.astype(F32) * scale).astype(BF16), head_dim, heads, 0)
            row = lax.broadcasted_iota(jnp.int32, tile.shape, 0) + c * QT
            tile = jnp.where(row < live, tile, jnp.zeros_like(tile))
            d_st = stacked(tile, head_dim, heads, hw)
            tile_t = tile.astype(F32).T
            q_cols = stacked_columns(tile_t * scale, head_dim, heads, 0)
            d_cols = stacked_columns(tile_t, head_dim, heads, hw)
            keys = [
                kv[pl.ds(pl.multiple_of(base + t, blk), KT), :] for t in range(0, slots, KT)
            ]
            scores = [dot(k, q_cols) for k in keys]
            grads = [dot(k, d_cols) for k in keys]
            flush(jnp.maximum(c - 1, 0))
            right[0:span, :] = q_st
            right[span:2 * span, :] = d_st
            probs = probs_of(scores, live, shifted)
            delta = functools.reduce(
                jnp.add, [jnp.sum(p * g, axis=0, keepdims=True) for p, g in zip(probs, grads)]
            )
            for t, (p, g) in enumerate(zip(probs, grads)):
                both[t * KT:(t + 1) * KT, 0:span] = (p * (g - delta)).astype(BF16)
                both[t * KT:(t + 1) * KT, span:2 * span] = p.astype(BF16)
            return carry

        chunks = (live + QT - 1) // QT
        lax.fori_loop(0, chunks, chunk, 0)
        flush(chunks - 1)
        dkv[pl.ds(base, slots), :] = acc[0:slots, :].astype(BF16)

    each_patch(1, groups, blk, at_ref, small, patch)

    for side in range(2):
        def back(b, g, r):
            at = pl.multiple_of(at_ref[1, b] * blk, blk)
            out_ref[g, pl.ds(r, blk), :] = dkv[pl.ds(at, blk), :]
            to = r + rows - side * half
            out_ref[g, pl.ds(to, blk), side * hw:(side + 1) * hw] = dq[pl.ds(at, blk), :]

        each_block(groups, per_group, blk, back, side * per_group // 2, per_group // 2)


def mix_kernel(groups, hw, att_ref, rows_ref, wproj_ref, out_ref, a_ref):
    half = a_ref.shape[0] // 2
    for g in range(groups):
        a_ref[0:half, g * hw:(g + 1) * hw] = att_ref[g, :, 0:hw]
        a_ref[half:2 * half, g * hw:(g + 1) * hw] = att_ref[g, :, hw:2 * hw]
    mixed = rows_ref[...].astype(F32) + dot(a_ref[...], wproj_ref[...])
    out_ref[...] = mixed.astype(BF16)


def input_grad_kernel(
    groups, hw, pick_ref, dqkv_ref, rows_ref, up_ref, gain_ref, wqkv_ref, out_ref, y_ref
):
    rows, width = up_ref.shape
    half = rows // 2
    for g in range(groups):
        low = g * hw
        y_ref[:, width + low:width + low + hw] = dqkv_ref[g, 0:rows, 0:hw]
        y_ref[:, 2 * width + low:2 * width + low + hw] = dqkv_ref[g, 0:rows, hw:2 * hw]
        y_ref[0:half, low:low + hw] = dqkv_ref[g, rows:rows + half, 0:hw]
        y_ref[half:rows, low:low + hw] = dqkv_ref[g, rows:rows + half, hw:2 * hw]
    grad = dot(y_ref[...], wqkv_ref[...], NT) * gain_ref[...]
    center, inv = centered(rows_ref[0].astype(F32))
    unit = center * inv
    mean = jnp.mean(grad, axis=-1, keepdims=True)
    along = jnp.mean(grad * unit, axis=-1, keepdims=True)
    pulled = inv * (grad - mean - unit * along)
    out_ref[...] = (up_ref[...].astype(F32) + pulled).astype(BF16)


def call(kernel, out_shape, operands, scratch=(), smem=0, cost=None, name=None, picked=None):
    specs = [pl.BlockSpec(memory_space=pltpu.SMEM)] * smem
    specs += [pl.BlockSpec(memory_space=pltpu.VMEM)] * (len(operands) - smem)
    kwargs = dict(
        out_shape=jax.ShapeDtypeStruct(out_shape, BF16),
        cost_estimate=pl.CostEstimate(flops=cost[0], bytes_accessed=cost[1], transcendentals=0),
        compiler_params=pltpu.CompilerParams(vmem_limit_bytes=VMEM_LIMIT),
        name=name,
    )
    if picked is None:
        return pl.pallas_call(
            kernel,
            in_specs=specs,
            out_specs=pl.BlockSpec(memory_space=pltpu.VMEM),
            scratch_shapes=list(scratch),
            **kwargs,
        )(*operands)

    def whole(shape):
        return pl.BlockSpec(shape, lambda i, pick: (0,) * len(shape))

    specs = [whole(o.shape) for o in operands[1:]]
    stash = operands[picked]
    specs[picked - 1] = pl.BlockSpec((1,) + stash.shape[1:], lambda i, pick: (pick[0], 0, 0))
    return pl.pallas_call(
        kernel,
        grid_spec=pltpu.PrefetchScalarGridSpec(
            num_scalar_prefetch=1,
            grid=(1,),
            in_specs=specs,
            out_specs=whole(out_shape),
            scratch_shapes=list(scratch),
        ),
        **kwargs,
    )(*operands)


def places(owners, groups):
    count = owners.shape[1]
    key = owners * count + jnp.arange(count, dtype=jnp.int32)
    bounds = jnp.broadcast_to(jnp.arange(groups + 1, dtype=jnp.int32) * count, (2, groups + 1))
    marks = jnp.concatenate([key, bounds], axis=1)
    return jnp.sum((key[:, None, :] < marks[:, :, None]).astype(jnp.int32), axis=2)


def swap(value):
    return lax.all_to_all(value, "space", split_axis=0, concat_axis=0, tiled=True)


def on_device(
    act_in, stash, plan, grad_in, fwd_owner, stash_owner, ln_gain, qkv_weight, proj_weight
):
    groups = lax.axis_size("space")
    rows_in = act_in[0]
    rows, width = rows_in.shape
    head_dim = width // HEADS
    hw = width // groups
    blk = rows // groups
    heads = hw // head_dim
    total = groups * rows
    span = heads * QT
    w_qkv = qkv_weight[0]
    w_proj = proj_weight[0]
    stored = stash[0]
    upstream = grad_in[0]
    stored_owners = lax.dynamic_index_in_dim(stash_owner[0], plan[0], 0, keepdims=False)
    mine = jnp.stack([fwd_owner[0], stored_owners]).reshape(2, groups, blk)[:, :, 0]
    owner_rows = jnp.pad(mine.astype(BF16), ((0, 14), (0, 2 * hw - groups)))

    sent_b = call(
        functools.partial(project_grad_kernel, groups, hw),
        (groups, 2 * rows + 16, 2 * hw),
        (plan, stored, upstream, ln_gain, w_qkv, w_proj, owner_rows),
        [pltpu.VMEM((rows, 3 * width), BF16), pltpu.VMEM((rows, width), BF16)],
        cost=(8 * rows * width * width, 6 * 1024 * 1024),
        name="project_grad",
        picked=1,
    )
    got_b = swap(sent_b)
    sent = call(
        functools.partial(project_kernel, groups, hw),
        (groups, 3 * rows // 2, 2 * hw),
        (rows_in, ln_gain, w_qkv),
        [pltpu.VMEM((rows, 3 * width), BF16)],
        cost=(6 * rows * width * width, 5 * 1024 * 1024),
        name="project",
    )
    got = swap(sent)
    owners = got_b[:, 2 * rows:2 * rows + 2, 0:groups].astype(jnp.int32)
    at = places(owners.transpose(1, 0, 2).reshape(2, groups * groups), groups)
    grads = call(
        functools.partial(attend_grad_kernel, groups, blk, hw, head_dim),
        (groups, 3 * rows // 2, 2 * hw),
        (at, got_b),
        [
            pltpu.VMEM((total + KT, 2 * hw), BF16),
            pltpu.VMEM((total + KT, 2 * hw), BF16),
            pltpu.VMEM((total + KT, hw), BF16),
            pltpu.VMEM((total + KT, 2 * hw), BF16),
            pltpu.VMEM((2 * hw, PATCH), BF16),
            pltpu.VMEM((PATCH, 2 * span), BF16),
            pltpu.VMEM((PATCH, 2 * hw), F32),
            pltpu.VMEM((2 * span, 2 * hw), BF16),
        ],
        smem=1,
        cost=(30_000_000_000, 4 * 1024 * 1024),
        name="attend_grad",
    )
    grads, got = lax.optimization_barrier((grads, got))
    ret_grads = swap(grads)
    attended = call(
        functools.partial(attend_kernel, groups, blk, hw, head_dim),
        (groups, rows // 2, 2 * hw),
        (at, got),
        [
            pltpu.VMEM((total + KT, 2 * hw), BF16),
            pltpu.VMEM((total + KT, 2 * hw), BF16),
            pltpu.VMEM((total + KT, hw), BF16),
            pltpu.VMEM((2 * hw, PATCH), BF16),
            pltpu.VMEM((PATCH, span), BF16),
        ],
        smem=1,
        cost=(20_000_000_000, 3 * 1024 * 1024),
        name="attend",
    )
    ret_grads, attended = lax.optimization_barrier((ret_grads, attended))
    ret = swap(attended)
    input_grad = call(
        functools.partial(input_grad_kernel, groups, hw),
        (rows, width),
        (plan, ret_grads, stored, upstream, ln_gain, w_qkv),
        [pltpu.VMEM((rows, 3 * width), BF16)],
        cost=(6 * rows * width * width, 5 * 1024 * 1024),
        name="input_grad",
        picked=2,
    )
    grad_out = passed_along(input_grad[None], "section", -1)
    mixed = call(
        functools.partial(mix_kernel, groups, hw),
        (rows, width),
        (ret, rows_in, w_proj),
        [pltpu.VMEM((rows, width), BF16)],
        cost=(2 * rows * width * width, 2 * 1024 * 1024),
        name="mix",
    )
    act_out = passed_along(mixed[None], "section", 1)
    return (act_out, grad_out)


def solution(mesh):
    in_specs = (
        P("section", "space", None),
        P("section", None, "space", None),
        P("section"),
        P("section", "space", None),
        P("section", "space"),
        P("section", None, "space"),
        P("section", None),
        P("section", None, None),
        P("section", None, None),
    )
    out_specs = (P("section", "space", None), P("section", "space", None))
    return jax.shard_map(
        on_device, mesh=mesh, in_specs=in_specs, out_specs=out_specs, check_vma=False
    )
```
